256 devices in a mesh: prow: 8 (over x, core), pcol: 32 (over y, z).
Axes of the slice: x: 4, y: 4, z: 8, core: 2. Of those that a mesh axis runs over, the one named last changes fastest.
Arguments:
- matrix: float32 [16384, 20480], P('prow', 'pcol'), may hold values from -6 to 6
- pivots: int32 [512], replicated, may hold values from 0 to 16383, as said below
- lower_inverse: float32 [512, 512], replicated, as said below
- upper_inverse: float32 [512, 512], replicated, as said below
Outputs:
- factored: float32 [16384, 20480], P('prow', 'pcol')
The draws below stay inside these ranges and needn't reach their ends.
Inputs may be any that keep to these rules, and one draw needn't show every extreme that they name: The 512 pivots are distinct. `lower_inverse`: unit diagonal, zeros above it. `upper_inverse`: zeros below the diagonal, a positive diagonal.
All inputs are finite; a program needn't handle non-finite values.
Results may differ from the reference program's by a relative error of at most 0.00005.
Values sent between devices are 32-bit elements; how exact they have to be, the bound alone decides.
A program may use at most 128 MiB of HBM per device.

```python
import jax
import jax.numpy as jnp
from jax import lax

NB = 512
ROWS = 16384
COLS = 20480


def draw_pivots(key, part):
    inner_key = jax.random.fold_in(key, 11)
    order_key = jax.random.fold_in(key, 23)
    inner = 1 + jax.random.permutation(inner_key, ROWS - 2)[:NB - 2]
    ends = jnp.array([0, ROWS - 1], dtype=jnp.int32)
    chosen = jnp.concatenate([ends, inner.astype(jnp.int32)], axis=0)
    placed = jax.random.permutation(order_key, NB)
    return chosen[placed].astype(jnp.int32)


def draw_lower_inverse(key, part):
    entries = jax.random.normal(key, (NB, NB), jnp.float32)
    strict = jnp.tril(entries, -1) * NB ** (-0.5)
    return (strict + jnp.eye(NB, dtype=jnp.float32)).astype(jnp.float32)


def draw_upper_inverse(key, part):
    first_key, second_key = jax.random.split(key)
    entries = jax.random.normal(first_key, (NB, NB), jnp.float32)
    diag = jnp.exp(jax.random.uniform(second_key, (NB,), jnp.float32, 0.0, jnp.log(2.0)))
    strict = jnp.triu(entries, 1) * NB ** (-0.5)
    return (0.05 * (strict + jnp.diag(diag))).astype(jnp.float32)


def block_scale(own_key, extent, pieces, low, largest):
    def one(position, blocks):
        steps = jax.random.uniform(jax.random.fold_in(jax.random.fold_in(own_key, 6), position), (blocks,), jnp.float32, low / len(pieces), largest / len(pieces))
        return jnp.repeat(jnp.exp(steps), extent[position] // blocks).reshape((-1,) + (1,) * (len(extent) - position - 1))

    factor_of = one(*pieces[0])
    for cut in pieces[1:]:
        factor_of = factor_of * one(*cut)
    return factor_of


def gaussian(rng, shape, deviation, bound, pieces=(), held_as=jnp.bfloat16):
    drawn = deviation * jax.random.normal(rng, shape, jnp.float32)
    if pieces:
        drawn = drawn * block_scale(rng, shape, pieces, -0.22, 0.18)
    return jnp.clip(drawn, -bound, bound).astype(held_as)


def setup_inputs(seed: int = 0) -> dict:
    splits = jax.random.split(jax.random.key(seed), 5)
    return {
        "matrix": gaussian(splits[0], (ROWS, COLS), 1.0, 6.0, ((0, 8), (1, 32)), jnp.float32),
        "pivots": draw_pivots(jax.random.fold_in(splits[4], 71), 0),
        "lower_inverse": draw_lower_inverse(jax.random.fold_in(splits[4], 71), 0),
        "upper_inverse": draw_upper_inverse(jax.random.fold_in(splits[4], 71), 0),
    }


def row_sources(pivots, panel_width):
    below = pivots >= panel_width
    vac_rank = jnp.cumsum(below.astype(jnp.int32)) - 1
    slot_ids = jnp.arange(panel_width, dtype=jnp.int32)
    chosen_top = jnp.any(pivots[:, None] == slot_ids[None, :], axis=0)
    freed_rows = jnp.logical_not(chosen_top)
    freed_rank = jnp.cumsum(freed_rows.astype(jnp.int32)) - 1
    pairing = freed_rows[None, :] & (freed_rank[None, :] == vac_rank[:, None])
    source_rows = jnp.sum(jnp.where(pairing, slot_ids[None, :], 0), axis=1).astype(jnp.int32)
    return below, source_rows


def reference(matrix, pivots, lower_inverse, upper_inverse):
    below, source_rows = row_sources(pivots, NB)
    row_order = jnp.arange(ROWS, dtype=jnp.int32)
    row_order = row_order.at[:NB].set(pivots)
    targets = jnp.where(below, pivots, ROWS).astype(jnp.int32)
    row_order = row_order.at[targets].set(source_rows, mode="drop")
    swapped = jnp.take(matrix, row_order, axis=0)
    u_rows = jnp.dot(lower_inverse, swapped[:NB], precision=lax.Precision.HIGHEST)
    lower_factor = jnp.dot(swapped[NB:, :NB], upper_inverse, precision=lax.Precision.HIGHEST)
    trailing = swapped[NB:, NB:] - jnp.dot(lower_factor, u_rows[:, NB:], precision=lax.Precision.HIGHEST)
    upper_band = jnp.concatenate([swapped[:NB, :NB], u_rows[:, NB:]], axis=1)
    lower_band = jnp.concatenate([lower_factor, trailing], axis=1)
    return jnp.concatenate([upper_band, lower_band], axis=0)
```

```python
import jax
import jax.numpy as jnp
from jax import lax
from jax.experimental import pallas as pl
from jax.experimental.pallas import tpu as pltpu
from jax.sharding import PartitionSpec as P

MESH = pl.DeviceIdType.MESH
F32 = jnp.float32
BF16 = jnp.bfloat16

OUT_TREE = (83, 2137, 73, 73, 65, 64, 64, 280, 1763, 729, 1243, 219, 88, 88, 1691, 1560,
            531, 512, 1683, 659, 83, 1555, 1747, 521, 1172, 658, 658, 74, 74, 1106, 1042, 1042)
DEPTH = (0, 13079, 17446, 21813, 26180, 21843, 17506, 13169, 4915, 9766, 13623, 17990, 22357, 18020, 13683, 9826,
         8772, 21301, 17510, 21847, 26214, 21877, 17510, 21331, 12629, 16966, 21303, 25670, 30037, 25700, 21363, 16996)
MAX_DEPTH = 7
CHUNKS = 32
HOP = 6
ROOT_LAG = 2
NB, ROWS, COLS = 512, 2048, 640
CHUNK = ROWS // (4 * CHUNKS)
STEPS = CHUNKS + HOP * MAX_DEPTH
GATHER_STEPS = 16
HALF, PIECE = NB // 2, NB // 8
TILE = 256


def split(x):
    high = x.astype(BF16)
    return high, (x - high.astype(F32)).astype(BF16)


def dot3(ah, al, bh, bl):
    return (
        jnp.dot(ah, bl, preferred_element_type=F32)
        + jnp.dot(al, bh, preferred_element_type=F32)
        + jnp.dot(ah, bh, preferred_element_type=F32)
    )


def pick(values, index):
    out = jnp.int32(0)
    for i, v in enumerate(values):
        out = jnp.where(index == i, jnp.int32(v), out)
    return out


def exchange(piv, m_hbm, li_ref, ui_ref, l_hbm, top_ref, u_ref, r_ref,
             m_ref, l_ref, g_ref, a0_ref, h_ref, a1_ref, nt_ref, uih, uil,
             load_sem, send_sem, recv_sem, out_sem, a_send, a_recv, b_send, b_recv):
    row = lax.axis_index("prow")
    col = lax.axis_index("pcol")
    x, core = lax.div(row, 2), lax.rem(row, 2)
    y, z = lax.div(col, 8), lax.rem(col, 8)
    near = [lax.rem(y + 1, 4) * 8 + z, lax.rem(y + 3, 4) * 8 + z,
            y * 8 + lax.rem(z + 1, 8), y * 8 + lax.rem(z + 7, 8)]
    root = col == 0
    partner = x * 2 + 1 - core

    barrier = pltpu.get_barrier_semaphore()
    for n in near:
        pl.semaphore_signal(barrier, inc=1, device_id={"pcol": n}, device_id_type=MESH)
    for i in range(1, 8):
        pl.semaphore_signal(barrier, inc=1, device_id={"prow": lax.rem(row + i, 8)}, device_id_type=MESH)

    def load(b):
        rows = pl.ds(pl.multiple_of(b * 128, 128), 128)
        return pltpu.make_async_copy(m_hbm.at[rows], m_ref.at[rows], load_sem.at[b])

    for b in range(16):
        load(b).start()

    trees = pick(OUT_TREE, col)
    depths = pick(DEPTH, col)
    tree = [lax.rem(lax.div(trees, 8**i), 8) for i in range(4)]
    lag = [jnp.where(root, ROOT_LAG, lax.rem(lax.div(depths, 16**i), 16) * HOP) for i in range(4)]
    out_lag = [jnp.where(t == 0, lag[0], jnp.where(t == 1, lag[1], jnp.where(t == 2, lag[2], lag[3]))) for t in tree]

    def chunk(t, k):
        return pl.ds(pl.multiple_of(k * (4 * CHUNK) + t * CHUNK, CHUNK), CHUNK)

    def to_row(src, dst, sems, j, target):
        return pltpu.make_async_remote_copy(
            src_ref=src, dst_ref=dst, send_sem=sems[0].at[j], recv_sem=sems[1].at[j],
            device_id={"prow": target}, device_id_type=MESH)

    @pl.when(root)
    def _():
        high, low = split(ui_ref[...])
        uih[...] = high
        uil[...] = low

    @pl.when(jnp.logical_not(root))
    def _():
        for b in range(16):
            load(b).wait()

    pl.semaphore_wait(barrier, 11)

    mine = pl.ds(pl.multiple_of(core * HALF, HALF), HALF)
    other = pl.ds(pl.multiple_of((1 - core) * HALF, HALF), HALF)
    my_piece = pl.ds(pl.multiple_of(core * HALF + x * PIECE, PIECE), PIECE)
    a_sems = (a_send, a_recv)
    b_sems = (b_send, b_recv)
    a0 = to_row(g_ref.at[other], a0_ref, a_sems, 0, partner)
    a1, a2 = [], []
    for i in range(3):
        peer = lax.rem(x + 3 - i, 4)
        rows = pl.ds(pl.multiple_of(peer * PIECE, PIECE), PIECE)
        a1.append(to_row(h_ref.at[rows], a1_ref.at[i], a_sems, 1 + i, peer * 2 + core))
        a2.append(to_row(nt_ref.at[my_piece], nt_ref.at[my_piece], a_sems, 4 + i, peer * 2 + core))
    a3 = to_row(nt_ref.at[mine], nt_ref.at[mine], a_sems, 7, partner)
    first, second = pl.ds(0, HALF), pl.ds(HALF, HALF)
    b_whole = to_row(r_ref, r_ref, b_sems, 0, 1)
    b_part = [to_row(r_ref.at[h], r_ref.at[h], b_sems, j, t)
              for h, j, t in ((first, 1, 2), (second, 2, 7), (second, 3, 3), (first, 4, 6))]
    b_relay_a = to_row(r_ref.at[first], r_ref.at[first], b_sems, 1, 4)
    b_relay_b = to_row(r_ref.at[second], r_ref.at[second], b_sems, 2, 5)

    receives = ((2, 1, first), (7, 2, second), (3, 3, second), (6, 4, first), (4, 1, first), (5, 2, second))

    def body(s, carry):
        @pl.when(root & (s < 16))
        def _():
            load(s).wait()
            rows = pl.ds(pl.multiple_of(s * 128, 128), 128)
            ph, plo = split(m_ref[rows, :NB])
            l_ref[rows, :] = dot3(ph, plo, uih[...], uil[...])

        for t in range(4):
            k = s - lag[t]

            @pl.when((k >= 0) & (k < CHUNKS))
            def _(t=t, k=k):
                part = l_ref.at[chunk(t, k)]

                @pl.when(jnp.logical_not(root))
                def _():
                    pltpu.make_async_copy(part, part, recv_sem.at[t, k]).wait()

        for d in range(4):
            k = s - out_lag[d]

            @pl.when((tree[d] < 4) & (k >= 0) & (k < CHUNKS))
            def _(d=d, k=k):
                part = l_ref.at[chunk(tree[d], k)]
                pltpu.make_async_remote_copy(
                    src_ref=part, dst_ref=part, send_sem=send_sem.at[d, k], recv_sem=recv_sem.at[tree[d], k],
                    device_id={"pcol": near[d]}, device_id_type=MESH).start()

        for t in range(4):
            k = s - lag[t]

            @pl.when((k >= 0) & (k < CHUNKS))
            def _(t=t, k=k):
                pltpu.make_async_copy(l_ref.at[chunk(t, k)], l_hbm.at[chunk(t, k)], out_sem).start()

        @pl.when((s >= 16) & (s < 16 + GATHER_STEPS))
        def _():
            for i in range(NB // GATHER_STEPS):
                j = (s - 16) * (NB // GATHER_STEPS) + i
                at = piv[j] - row * ROWS
                inside = (at >= 0) & (at < ROWS)
                picked = m_ref[pl.ds(jnp.clip(at, 0, ROWS - 1), 1), :]
                g_ref[pl.ds(j, 1), :] = jnp.where(inside, picked, 0.0)

        @pl.when(s == 33)
        def _():
            a0.start()

        @pl.when(s == 37)
        def _():
            a0.wait()
            h_ref[...] = g_ref[mine, :] + a0_ref[...]

        @pl.when(s == 38)
        def _():
            for c in a1:
                c.start()

        @pl.when(s == 48)
        def _():
            for c in a1:
                c.wait()
            nt_ref[my_piece, :] = h_ref[pl.ds(pl.multiple_of(x * PIECE, PIECE), PIECE), :] + a1_ref[0] + a1_ref[1] + a1_ref[2]

        @pl.when(s == 49)
        def _():
            for c in a2:
                c.start()

        @pl.when(s == 60)
        def _():
            for c in a2:
                c.wait()
            a3.start()

        @pl.when(s == 64)
        def _():
            a3.wait()
            lh, ll = split(li_ref[...])
            nh, nl = split(nt_ref[...])
            u = dot3(lh, ll, nh, nl)
            u_ref[...] = u
            top_ref[...] = u

            @pl.when(root)
            def _():
                top_ref[:, :NB] = nt_ref[:, :NB]

        @pl.when((s == 65) & (row == 0))
        def _():
            lh, ll = split(l_ref[:NB, :])
            uh, ul = split(u_ref[...])
            r_ref[...] = m_ref[:NB, :] - dot3(lh, ll, uh, ul)

            @pl.when(root)
            def _():
                r_ref[:, :NB] = l_ref[:NB, :]

        @pl.when((s == 66) & (row == 0))
        def _():
            for c in b_part:
                c.start()
            b_whole.start()

        return carry

    lax.fori_loop(0, STEPS + 1, body, 0)

    for device, sem, rows in receives:
        @pl.when(row == device)
        def _(sem=sem, rows=rows):
            pltpu.make_async_copy(r_ref.at[rows], r_ref.at[rows], b_recv.at[sem]).wait()

        if device == 2:
            @pl.when(row == device)
            def _():
                b_relay_a.start()
        if device == 7:
            @pl.when(row == device)
            def _():
                b_relay_b.start()

    @pl.when(row == 1)
    def _():
        b_whole.wait_recv()

    for device, sem, rows in receives:
        @pl.when(row == device)
        def _(rows=rows, device=device):
            own = to_row(r_ref.at[rows], r_ref.at[rows], b_sems, 5, device ^ 1)
            own.start()
            own.wait_send()
            back = second if rows is first else first
            to_row(r_ref.at[back], r_ref.at[back], b_sems, 5, device ^ 1).wait_recv()

    @pl.when(row == 0)
    def _():
        for c in b_part:
            c.wait_send()
        b_whole.wait_send()

    @pl.when(row == 2)
    def _():
        b_relay_a.wait_send()

    @pl.when(row == 7)
    def _():
        b_relay_b.wait_send()

    def drain(k, carry):
        for d in range(4):
            @pl.when(tree[d] < 4)
            def _(d=d):
                part = l_ref.at[chunk(tree[d], k)]
                pltpu.make_async_copy(part, part, send_sem.at[d, k]).wait()
        return carry

    lax.fori_loop(0, CHUNKS, drain, 0)
    pltpu.make_async_copy(l_ref, l_hbm, out_sem).wait()


def update(at_rows, at_src, bounds, m_ref, l_ref, u_ref, top_ref, r_ref, o_ref, uh, ul):
    b = pl.program_id(0)
    row = lax.axis_index("prow")
    col = lax.axis_index("pcol")

    @pl.when(b == 0)
    def _():
        high, low = split(u_ref[...])
        uh[...] = high
        ul[...] = low

    top = (row == 0) & (b < NB // TILE)

    @pl.when(top)
    def _():
        o_ref[...] = top_ref[pl.ds(pl.multiple_of(lax.rem(b, NB // TILE) * TILE, TILE), TILE), :]

    @pl.when(jnp.logical_not(top))
    def _():
        lh, ll = split(l_ref[...])
        o_ref[...] = m_ref[...] - dot3(lh, ll, uh[...], ul[...])

        @pl.when(col == 0)
        def _():
            o_ref[:, :NB] = l_ref[...]

        def place(p, carry):
            o_ref[pl.ds(at_rows[p] - b * TILE, 1), :] = r_ref[pl.ds(at_src[p], 1), :]
            return carry

        lax.fori_loop(bounds[b], bounds[b + 1], place, 0)


def moves(pivots, row):
    slots = jnp.arange(NB, dtype=jnp.int32)
    below = pivots >= NB
    vacancy = jnp.sum((below[None, :] & (slots[None, :] <= slots[:, None])).astype(jnp.int32), axis=1) - 1
    freed = jnp.logical_not(jnp.any(pivots[:, None] == slots[None, :], axis=0))
    rank = jnp.sum((freed[None, :] & (slots[None, :] <= slots[:, None])).astype(jnp.int32), axis=1) - 1
    pairing = freed[None, :] & (rank[None, :] == vacancy[:, None])
    source = jnp.sum(jnp.where(pairing, slots[None, :], 0), axis=1)
    at = pivots - row * ROWS
    here = below & (at >= 0) & (at < ROWS)
    place = jnp.sum((here[None, :] & (at[None, :] < at[:, None])).astype(jnp.int32), axis=1)
    hit = here[None, :] & (place[None, :] == slots[:, None])
    at_rows = jnp.sum(jnp.where(hit, at[None, :], 0), axis=1)
    at_src = jnp.sum(jnp.where(hit, source[None, :], 0), axis=1)
    edges = jnp.arange(ROWS // TILE + 1, dtype=jnp.int32) * TILE
    bounds = jnp.sum((here[None, :] & (at[None, :] < edges[:, None])).astype(jnp.int32), axis=1)
    return at_rows, at_src, bounds


def local(matrix, pivots, lower_inverse, upper_inverse):
    at_rows, at_src, bounds = moves(pivots, lax.axis_index("prow"))
    vmem = pl.BlockSpec(memory_space=pltpu.VMEM)
    hbm = pl.BlockSpec(memory_space=pl.ANY)
    strip = jax.ShapeDtypeStruct((NB, COLS), F32)
    spread, top, u_rows, old = pl.pallas_call(
        exchange,
        out_shape=(jax.ShapeDtypeStruct((ROWS, NB), F32), strip, strip, strip),
        in_specs=[pl.BlockSpec(memory_space=pltpu.SMEM), hbm, vmem, vmem],
        out_specs=(hbm, vmem, vmem, vmem),
        scratch_shapes=[
            pltpu.VMEM((ROWS, COLS), F32),
            pltpu.VMEM((ROWS, NB), F32),
            pltpu.VMEM((NB, COLS), F32),
            pltpu.VMEM((HALF, COLS), F32),
            pltpu.VMEM((HALF, COLS), F32),
            pltpu.VMEM((3, PIECE, COLS), F32),
            pltpu.VMEM((NB, COLS), F32),
            pltpu.VMEM((NB, NB), BF16),
            pltpu.VMEM((NB, NB), BF16),
            pltpu.SemaphoreType.DMA((16,)),
            pltpu.SemaphoreType.DMA((4, CHUNKS)),
            pltpu.SemaphoreType.DMA((4, CHUNKS)),
            pltpu.SemaphoreType.DMA,
            pltpu.SemaphoreType.DMA((8,)),
            pltpu.SemaphoreType.DMA((8,)),
            pltpu.SemaphoreType.DMA((6,)),
            pltpu.SemaphoreType.DMA((6,)),
        ],
        compiler_params=pltpu.CompilerParams(collective_id=0, has_side_effects=True, vmem_limit_bytes=60 << 20),
        name="exchange",
    )(pivots, matrix, lower_inverse, upper_inverse)
    tile = lambda width: pl.BlockSpec((TILE, width), lambda b, *_: (b, 0))
    whole = pl.BlockSpec((NB, COLS), lambda b, *_: (0, 0))
    return pl.pallas_call(
        update,
        out_shape=jax.ShapeDtypeStruct((ROWS, COLS), F32),
        grid_spec=pltpu.PrefetchScalarGridSpec(
            num_scalar_prefetch=3,
            grid=(ROWS // TILE,),
            in_specs=[tile(COLS), tile(NB), whole, whole, whole],
            out_specs=tile(COLS),
            scratch_shapes=[pltpu.VMEM((NB, COLS), BF16), pltpu.VMEM((NB, COLS), BF16)],
        ),
        name="update",
    )(at_rows, at_src, bounds, matrix, spread, u_rows, top, old)


def solution(mesh):
    return jax.shard_map(
        local,
        mesh=mesh,
        in_specs=(P("prow", "pcol"), P(), P(), P()),
        out_specs=P("prow", "pcol"),
        check_vma=False,
    )
```

```python
import jax
import jax.numpy as jnp
from jax import lax
from jax.experimental import pallas as pl
from jax.experimental.pallas import tpu as pltpu
from jax.sharding import PartitionSpec as P

MESH = pl.DeviceIdType.MESH
F32 = jnp.float32
BF16 = jnp.bfloat16

OUT_TREE = (1035, 2048, 1048, 1024, 1026, 1042, 1042, 1298, 1760, 219, 728, 1051, 1051, 1562, 1627, 1690, 139, 1682, 522,
            1547, 1035, 1163, 1739, 128, 588, 65, 1609, 73, 1033, 1033, 713, 649)
DEPTH = (0, 424388, 551496, 678604, 837489, 702197, 566905, 431613, 145836, 289576, 424620, 551728, 710613, 575321,
         440029, 304985, 543024, 416429, 813616, 686772, 845657, 710365, 583257, 701909, 670893, 846121, 719285,
         814641, 973526, 838234, 702942, 829785)
MAX_DEPTH = 30
CHUNKS = 32
HOP = 5
NB, ROWS, COLS = 512, 2048, 640
CHUNK = ROWS // (4 * CHUNKS)
STEPS = CHUNKS + HOP * MAX_DEPTH // 4
GATHER_STEPS = 16
HALF, PIECE = NB // 2, NB // 8
TILE = 512
ROOT_LATE = 16
EXCHANGE_VMEM = 40 << 20
UPDATE_VMEM = 24 << 20


def split(x):
    high = x.astype(BF16)
    return high, (x - high.astype(F32)).astype(BF16)


def wide(x):
    high, low = split(x)
    return jnp.concatenate([high, low, high], axis=1)


def tall(ref, x, rows=0):
    n = x.shape[0]
    high, low = split(x)
    ref[rows : rows + n, :] = high
    ref[NB + rows : NB + rows + n, :] = high
    ref[2 * NB + rows : 2 * NB + rows + n, :] = low


def product(x, ref):
    return jnp.dot(wide(x), ref[...], preferred_element_type=F32)


def pick(values, index):
    out = jnp.int32(0)
    for i, v in enumerate(values):
        out = jnp.where(index == i, jnp.int32(v), out)
    return out


def exchange(piv, piv_hbm, m_hbm, li_hbm, ui_hbm, l_out, top_out, uu_out, ot_ref, lo_ref, list_ref, bound_ref,
             m_ref, l_ref, g_ref, a0_ref, h_ref, a1_ref, nt_ref, ui_tall, nt_tall, src_ref, piv_row, li_ref, ui_ref,
             top_ref, uu_ref, load_sem, in_sem, send_sem, recv_sem, out_sem, u_sem, a_send, a_recv, b_send, b_recv, c_send, c_recv):
    row = lax.axis_index("prow")
    col = lax.axis_index("pcol")
    x, core = lax.div(row, 2), lax.rem(row, 2)
    y, z = lax.div(col, 8), lax.rem(col, 8)
    near = [lax.rem(y + 1, 4) * 8 + z, lax.rem(y + 3, 4) * 8 + z,
            y * 8 + lax.rem(z + 1, 8), y * 8 + lax.rem(z + 7, 8)]
    root = col == 0
    partner = x * 2 + 1 - core

    barrier = pltpu.get_barrier_semaphore()
    for n in near:
        pl.semaphore_signal(barrier, inc=1, device_id={"pcol": n}, device_id_type=MESH)
    for i in range(1, 8):
        pl.semaphore_signal(barrier, inc=1, device_id={"prow": lax.rem(row + i, 8)}, device_id_type=MESH)

    def load(b):
        rows = pl.ds(pl.multiple_of(b * 128, 128), 128)
        return pltpu.make_async_copy(m_hbm.at[rows], m_ref.at[rows], load_sem.at[b])

    load(0).start()
    get_ui = pltpu.make_async_copy(ui_hbm, ui_ref, in_sem.at[0])
    get_li = pltpu.make_async_copy(li_hbm, li_ref, in_sem.at[1])
    get_piv = pltpu.make_async_copy(piv_hbm, piv_row, in_sem.at[2])
    get_ui.start()
    for b in range(1, 16):
        load(b).start()
    get_piv.start()
    get_li.start()

    trees = pick(OUT_TREE, col)
    depths = pick(DEPTH, col)
    tree = [lax.rem(lax.div(trees, 8**i), 8) for i in range(4)]
    lag = [lax.div(lax.rem(lax.div(depths, 32**i), 32) * HOP, 4) for i in range(4)]
    last_lag = jnp.maximum(jnp.maximum(lag[0], lag[1]), jnp.maximum(lag[2], lag[3]))
    out_lag = [jnp.where(t == 0, lag[0], jnp.where(t == 1, lag[1], jnp.where(t == 2, lag[2], lag[3]))) for t in tree]

    def chunk(t, k):
        return pl.ds(pl.multiple_of(k * (4 * CHUNK) + t * CHUNK, CHUNK), CHUNK)

    def to_row(src, dst, sems, j, target):
        return pltpu.make_async_remote_copy(
            src_ref=src, dst_ref=dst, send_sem=sems[0].at[j], recv_sem=sems[1].at[j],
            device_id={"prow": target}, device_id_type=MESH)

    get_ui.wait()

    @pl.when(root)
    def _():
        tall(ui_tall, ui_ref[...])

    pl.semaphore_wait(barrier, 11)

    mine = pl.ds(pl.multiple_of(core * HALF, HALF), HALF)
    other = pl.ds(pl.multiple_of((1 - core) * HALF, HALF), HALF)
    my_piece = pl.ds(pl.multiple_of(core * HALF + x * PIECE, PIECE), PIECE)
    a_sems = (a_send, a_recv)
    b_sems = (b_send, b_recv)
    a0 = to_row(g_ref.at[other], a0_ref, a_sems, 0, partner)
    a1, a2 = [], []
    for i in range(3):
        peer = lax.rem(x + 3 - i, 4)
        rows = pl.ds(pl.multiple_of(peer * PIECE, PIECE), PIECE)
        a1.append(to_row(h_ref.at[rows], a1_ref.at[i], a_sems, 1 + i, peer * 2 + core))
        a2.append(to_row(nt_ref.at[my_piece], nt_ref.at[my_piece], a_sems, 4 + i, peer * 2 + core))
    a3 = to_row(nt_ref.at[mine], nt_ref.at[mine], a_sems, 7, partner)
    first, second = pl.ds(0, HALF), pl.ds(HALF, HALF)
    quarter = [pl.ds(i * 128, 128) for i in range(4)]

    class Stream:
        def __init__(self, src, dst, sems):
            def part(ref, rows, j, target):
                return to_row(ref.at[rows], dst.at[rows], sems, j, target)

            self.first = [part(src, quarter[i], 1 + i, 2 if i < 2 else 7) for i in range(4)]
            self.rest = [part(src, second, 5, 3), part(src, first, 6, 6), part(src, pl.ds(0, NB), 0, 1)]
            self.relay = [part(dst, quarter[i], 1 + i, 4 if i < 2 else 5) for i in range(4)]
            self.have = {2: ([], first), 7: ([], second), 4: (self.relay[:2], first), 5: (self.relay[2:], second),
                         6: (self.rest[1:2], first), 3: (self.rest[:1], second)}
            self.swap = {d: part(dst, h, 7, d ^ 1) for d, (_, h) in self.have.items()}
            self.back = {d: part(dst, second if h is first else first, 7, d ^ 1) for d, (_, h) in self.have.items()}

        def start(self):
            for c in self.first + self.rest:
                c.start()

        def pass_on(self, i):
            for j, device in ((i, 2), (2 + i, 7)):
                @pl.when(row == device)
                def _(j=j):
                    self.first[j].wait_recv()
                    self.relay[j].start()

        def start_swap(self):
            for d, (waits, _) in self.have.items():
                @pl.when(row == d)
                def _(d=d, waits=waits):
                    for c in waits:
                        c.wait_recv()
                    self.swap[d].start()

        def finish(self):
            for d in self.have:
                @pl.when(row == d)
                def _(d=d):
                    self.swap[d].wait_send()
                    self.back[d].wait_recv()

            @pl.when(row == 1)
            def _():
                self.rest[2].wait_recv()

            @pl.when(row == 0)
            def _():
                for c in self.first + self.rest:
                    c.wait_send()

            for i in range(4):
                @pl.when(row == (2, 7)[i // 2])
                def _(i=i):
                    self.relay[i].wait_send()

    old_top = Stream(m_ref, ot_ref, b_sems)
    old_factor = Stream(l_ref, lo_ref, (c_send, c_recv))
    own_top = pltpu.make_async_copy(m_ref.at[pl.ds(0, NB)], ot_ref, in_sem.at[3])
    own_factor = pltpu.make_async_copy(l_ref.at[pl.ds(0, NB)], lo_ref, in_sem.at[4])
    put_top = pltpu.make_async_copy(top_ref, top_out, u_sem.at[0])
    put_uu = pltpu.make_async_copy(uu_ref, uu_out, u_sem.at[1])
    factor_step = jnp.where(root, 12, last_lag + NB // (4 * CHUNK))

    @pl.when(row == 0)
    def _():
        for b in range(4):
            load(b).wait()
        old_top.start()
        own_top.start()

    for b in range(16):
        @pl.when(jnp.logical_not(root) & ((row > 0) | (b >= 4)))
        def _(b=b):
            load(b).wait()

        if b < 4:
            @pl.when(root & (row > 0))
            def _(b=b):
                load(b).wait()

    get_piv.wait()
    pr = piv_row[...].astype(F32)
    lane = lax.broadcasted_iota(jnp.int32, (1, NB), 1)
    here_at = pr - (row * ROWS).astype(F32)
    here = (pr >= NB) & (here_at >= 0) & (here_at < ROWS)
    here_at = jnp.where(here, here_at, float(2 * ROWS))

    def rank_vacancies():
        vacancy = jnp.where(pr >= NB, 1.0, 0.0)
        for i in range(9):
            vacancy = vacancy + jnp.where(lane >= 2**i, pltpu.roll(vacancy, 2**i, 1), 0.0)
        src_ref[3:4, :] = vacancy

    def column(v):
        return jnp.transpose(jnp.broadcast_to(v, (128, 128)), (1, 0))[:, :1]

    pl.when(jnp.logical_not(root))(rank_vacancies)

    def body(s, carry):
        pl.when(root & (s == 17))(rank_vacancies)

        @pl.when(root & (s < 16))
        def _():
            @pl.when(s == 3)
            def _():
                for b in range(4, 16):
                    load(b).wait()

            rows = pl.ds(pl.multiple_of(s * 128, 128), 128)
            l_ref[rows, :] = product(m_ref[rows, :NB], ui_tall)

        @pl.when(root & (s >= 1) & (s <= 16))
        def _():
            for u in range(2):
                k = 2 * (s - 1) + u
                for d in range(4):
                    @pl.when(tree[d] < 4)
                    def _(d=d, k=k):
                        part = l_ref.at[chunk(tree[d], k)]
                        pltpu.make_async_remote_copy(
                            src_ref=part, dst_ref=part, send_sem=send_sem.at[d, k], recv_sem=recv_sem.at[tree[d], k],
                            device_id={"pcol": near[d]}, device_id_type=MESH).start()

        @pl.when(jnp.logical_not(root))
        def _():
            for t in range(4):
                k = s - lag[t]

                @pl.when((k >= 0) & (k < CHUNKS))
                def _(t=t, k=k):
                    part = l_ref.at[chunk(t, k)]
                    pltpu.make_async_copy(part, part, recv_sem.at[t, k]).wait()

            for d in range(4):
                k = s - out_lag[d]

                @pl.when((tree[d] < 4) & (k >= 0) & (k < CHUNKS))
                def _(d=d, k=k):
                    part = l_ref.at[chunk(tree[d], k)]
                    pltpu.make_async_remote_copy(
                        src_ref=part, dst_ref=part, send_sem=send_sem.at[d, k], recv_sem=recv_sem.at[tree[d], k],
                        device_id={"pcol": near[d]}, device_id_type=MESH).start()

            for t in range(4):
                k = s - lag[t]

                @pl.when((k >= 0) & (k < CHUNKS))
                def _(t=t, k=k):
                    pltpu.make_async_copy(l_ref.at[chunk(t, k)], l_out.at[chunk(t, k)], out_sem).start()

        @pl.when((s == factor_step) & (row == 0))
        def _():
            old_factor.start()
            own_factor.start()

        for i in range(2):
            @pl.when(s == factor_step + 11 + 4 * i)
            def _(i=i):
                old_factor.pass_on(i)

            @pl.when(s == 14 + 4 * i)
            def _(i=i):
                old_top.pass_on(i)

        @pl.when(s == 36)
        def _():
            old_top.start_swap()

        at_step = s - jnp.where(root, ROOT_LATE, 0)

        @pl.when((at_step >= 0) & (at_step < GATHER_STEPS))
        def _():
            for i in range(NB // GATHER_STEPS):
                j = at_step * (NB // GATHER_STEPS) + i
                at = piv[j] - row * ROWS
                inside = (at >= 0) & (at < ROWS)
                picked = m_ref[pl.ds(jnp.clip(at, 0, ROWS - 1), 1), :]
                g_ref[pl.ds(j, 1), :] = jnp.where(inside, picked, 0.0)

        def step(n):
            return pl.when(at_step == n)

        @step(17)
        def _():
            a0.start()

        @step(21)
        def _():
            a0.wait()
            h_ref[...] = g_ref[mine, :] + a0_ref[...]

        @step(22)
        def _():
            for c in a1:
                c.start()

        for q in range(4):
            @step(23 + q)
            def _(q=q):
                vacancy = src_ref[3:4, :]
                slot = (lax.broadcasted_iota(jnp.int32, (128, 1), 0) + 128 * q).astype(F32)
                chosen = jnp.sum(jnp.where(pr == slot, 1.0, 0.0), axis=1, keepdims=True)
                rank = slot - jnp.sum(jnp.where(pr <= slot, 1.0, 0.0), axis=1, keepdims=True)
                key = jnp.where(chosen > 0, -7.0, rank)
                found = jnp.sum(jnp.where(key == vacancy - 1, slot, 0.0), axis=0, keepdims=True)
                src_ref[0:1, :] = found if q == 0 else src_ref[0:1, :] + found

        for q in range(4):
            @step(27 + q)
            def _(q=q):
                cut = slice(128 * q, 128 * q + 128)
                at_col = column(here_at[:, cut])
                src_col = column(src_ref[0:1, cut])
                place = jnp.sum(jnp.where(here_at < at_col, 1.0, 0.0), axis=1, keepdims=True)
                place = jnp.where(at_col < ROWS, place, -7.0)
                code = jnp.sum(jnp.where(place == lane.astype(F32), at_col * NB + src_col, 0.0), axis=0, keepdims=True)
                edge = (lane[:, :128] * TILE).astype(F32)
                count = jnp.sum(jnp.where(at_col < edge, 1.0, 0.0), axis=0, keepdims=True)
                src_ref[1:2, :] = code if q == 0 else src_ref[1:2, :] + code
                src_ref[2:3, :128] = count if q == 0 else src_ref[2:3, :128] + count
                if q == 3:
                    list_ref[...] = src_ref[1:2, :].astype(jnp.int32)
                    bound_ref[...] = src_ref[2:3, :128].astype(jnp.int32)

        @step(42)
        def _():
            for c in a1:
                c.wait()
            nt_ref[my_piece, :] = h_ref[pl.ds(pl.multiple_of(x * PIECE, PIECE), PIECE), :] + a1_ref[0] + a1_ref[1] + a1_ref[2]

        @step(43)
        def _():
            for c in a2:
                c.start()

        @step(57)
        def _():
            for c in a2:
                c.wait()
            a3.start()

        @step(61)
        def _():
            a3.wait()
            get_li.wait()
            tall(nt_tall, nt_ref[...])

        for q in range(4):
            @step(62 + q)
            def _(q=q):
                cut = slice(128 * q, 128 * q + 128)
                u = product(li_ref[cut, :], nt_tall)
                top_ref[cut, :] = u
                tall(uu_ref, u, 128 * q)

                @pl.when(root)
                def _():
                    top_ref[cut, :NB] = nt_ref[cut, :NB]

        @step(66)
        def _():
            put_top.start()
            put_uu.start()

        return carry

    lax.fori_loop(0, STEPS + 1 + jnp.where(root, ROOT_LATE, 0), body, 0)

    @pl.when(root)
    def _():
        pltpu.make_async_copy(l_ref, l_out, out_sem).start()

    old_factor.start_swap()
    old_top.finish()
    old_factor.finish()

    @pl.when(row == 0)
    def _():
        own_top.wait()
        own_factor.wait()

    put_top.wait()
    put_uu.wait()

    def drain(k, carry):
        for d in range(4):
            @pl.when(tree[d] < 4)
            def _(d=d):
                part = l_ref.at[chunk(tree[d], k)]
                pltpu.make_async_copy(part, part, send_sem.at[d, k]).wait()
        return carry

    lax.fori_loop(0, CHUNKS, drain, 0)
    pltpu.make_async_copy(l_ref, l_out, out_sem).wait()


def update(code, bounds, m_ref, l_ref, uu_ref, top_ref, ot_ref, lo_ref, o_ref, lt_ref):
    b = pl.program_id(0)
    row = lax.axis_index("prow")
    col = lax.axis_index("pcol")
    top = (row == 0) & (b < NB // TILE)

    @pl.when(top)
    def _():
        o_ref[...] = top_ref[...]

    @pl.when(jnp.logical_not(top))
    def _():
        o_ref[...] = m_ref[...]
        lt_ref[...] = l_ref[...]

        def place(p, carry):
            at, source = lax.div(code[0, p], NB), lax.rem(code[0, p], NB)
            here, there = pl.ds(at - b * TILE, 1), pl.ds(source, 1)
            o_ref[here, :] = ot_ref[there, :]
            lt_ref[here, :] = lo_ref[there, :]
            return carry

        lax.fori_loop(bounds[0, b], bounds[0, b + 1], place, 0)
        o_ref[...] = o_ref[...] - product(lt_ref[...], uu_ref)

        @pl.when(col == 0)
        def _():
            o_ref[:, :NB] = lt_ref[...]


def local(matrix, pivots, lower_inverse, upper_inverse):
    vmem = pl.BlockSpec(memory_space=pltpu.VMEM)
    hbm = pl.BlockSpec(memory_space=pl.ANY)
    stay = pl.BlockSpec(memory_space=pltpu.MemorySpace.HBM)
    strip = jax.ShapeDtypeStruct((NB, COLS), F32)
    u_tall = jax.ShapeDtypeStruct((3 * NB, COLS), BF16)
    spread, top, u_tall, old, old_factor, code, bounds = pl.pallas_call(
        exchange,
        out_shape=(jax.ShapeDtypeStruct((ROWS, NB), F32), strip, u_tall, strip, jax.ShapeDtypeStruct((NB, NB), F32),
                   jax.ShapeDtypeStruct((1, NB), jnp.int32), jax.ShapeDtypeStruct((1, 128), jnp.int32)),
        in_specs=[pl.BlockSpec(memory_space=pltpu.SMEM), stay, stay, stay, stay],
        out_specs=(hbm, hbm, hbm, hbm, hbm, vmem, vmem),
        scratch_shapes=[
            pltpu.VMEM((ROWS, COLS), F32),
            pltpu.VMEM((ROWS, NB), F32),
            pltpu.VMEM((NB, COLS), F32),
            pltpu.VMEM((HALF, COLS), F32),
            pltpu.VMEM((HALF, COLS), F32),
            pltpu.VMEM((3, PIECE, COLS), F32),
            pltpu.VMEM((NB, COLS), F32),
            pltpu.VMEM((3 * NB, NB), BF16),
            pltpu.VMEM((3 * NB, COLS), BF16),
            pltpu.VMEM((8, NB), F32),
            pltpu.VMEM((1, NB), jnp.int32),
            pltpu.VMEM((NB, NB), F32),
            pltpu.VMEM((NB, NB), F32),
            pltpu.VMEM((NB, COLS), F32),
            pltpu.VMEM((3 * NB, COLS), BF16),
            pltpu.SemaphoreType.DMA((16,)),
            pltpu.SemaphoreType.DMA((5,)),
            pltpu.SemaphoreType.DMA((4, CHUNKS)),
            pltpu.SemaphoreType.DMA((4, CHUNKS)),
            pltpu.SemaphoreType.DMA,
            pltpu.SemaphoreType.DMA((2,)),
            *[pltpu.SemaphoreType.DMA((8,))] * 6,
        ],
        compiler_params=pltpu.CompilerParams(collective_id=0, has_side_effects=True, vmem_limit_bytes=EXCHANGE_VMEM),
        name="exchange",
    )(pivots, pivots.reshape(1, NB), *(pltpu.with_memory_space_constraint(v, pltpu.MemorySpace.HBM) for v in (matrix, lower_inverse, upper_inverse)))
    tile = lambda width: pl.BlockSpec((TILE, width), lambda b, *_: (b, 0))
    whole = lambda rows: pl.BlockSpec((rows, COLS), lambda b, *_: (0, 0))
    return pl.pallas_call(
        update,
        out_shape=jax.ShapeDtypeStruct((ROWS, COLS), F32),
        grid_spec=pltpu.PrefetchScalarGridSpec(
            num_scalar_prefetch=2,
            grid=(ROWS // TILE,),
            in_specs=[tile(COLS), tile(NB), whole(3 * NB), whole(NB), whole(NB), pl.BlockSpec((NB, NB), lambda b, *_: (0, 0))],
            out_specs=tile(COLS),
            scratch_shapes=[pltpu.VMEM((TILE, NB), F32)],
        ),
        compiler_params=pltpu.CompilerParams(vmem_limit_bytes=UPDATE_VMEM),
        name="update",
    )(code, bounds, matrix, spread, u_tall, top, old, old_factor)


def solution(mesh):
    return jax.shard_map(
        local,
        mesh=mesh,
        in_specs=(P("prow", "pcol"), P(), P(), P()),
        out_specs=P("prow", "pcol"),
        check_vma=False,
    )
```

```python
import jax
import jax.numpy as jnp
from jax import lax
from jax.experimental import pallas as pl
from jax.experimental.pallas import tpu as pltpu
from jax.sharding import PartitionSpec as P

MESH = pl.DeviceIdType.MESH
F32 = jnp.float32
BF16 = jnp.bfloat16

OUT_TREE = (1035, 2048, 1048, 1024, 1026, 1042, 1042, 1298, 1760, 219, 728, 1051, 1051, 1562, 1627, 1690, 139, 1682, 522,
            1547, 1035, 1163, 1739, 128, 588, 65, 1609, 73, 1033, 1033, 713, 649)
DEPTH = (0, 424388, 551496, 678604, 837489, 702197, 566905, 431613, 145836, 289576, 424620, 551728, 710613, 575321,
         440029, 304985, 543024, 416429, 813616, 686772, 845657, 710365, 583257, 701909, 670893, 846121, 719285,
         814641, 973526, 838234, 702942, 829785)
MAX_DEPTH = 30
CHUNKS = 32
HOP = 4
NB, ROWS, COLS = 512, 2048, 640
CHUNK = ROWS // (4 * CHUNKS)
STEPS = CHUNKS + HOP * MAX_DEPTH // 4
GATHER_STEPS = 16
HALF, PIECE = NB // 2, NB // 8
TILE = 512
ROOT_LATE = 16
EXCHANGE_VMEM = 40 << 20
UPDATE_VMEM = 24 << 20


def split(x):
    high = x.astype(BF16)
    return high, (x - high.astype(F32)).astype(BF16)


def wide(x):
    high, low = split(x)
    return jnp.concatenate([high, low, high], axis=1)


def tall(ref, x, rows=0):
    n = x.shape[0]
    high, low = split(x)
    ref[rows : rows + n, :] = high
    ref[NB + rows : NB + rows + n, :] = high
    ref[2 * NB + rows : 2 * NB + rows + n, :] = low


def product(x, ref):
    return jnp.dot(wide(x), ref[...], preferred_element_type=F32)


def pick(values, index):
    out = jnp.int32(0)
    for i, v in enumerate(values):
        out = jnp.where(index == i, jnp.int32(v), out)
    return out


def exchange(piv, piv_hbm, m_hbm, li_hbm, ui_hbm, l_out, top_out, uu_out, ot_ref, lo_ref, list_ref, bound_ref,
             m_ref, l_ref, g_ref, a0_ref, h_ref, a1_ref, nt_ref, ui_tall, nt_tall, src_ref, piv_row, li_ref, ui_ref,
             top_ref, uu_ref, load_sem, in_sem, send_sem, recv_sem, out_sem, u_sem, a_send, a_recv, b_send, b_recv, c_send, c_recv):
    row = lax.axis_index("prow")
    col = lax.axis_index("pcol")
    x, core = lax.div(row, 2), lax.rem(row, 2)
    y, z = lax.div(col, 8), lax.rem(col, 8)
    near = [lax.rem(y + 1, 4) * 8 + z, lax.rem(y + 3, 4) * 8 + z,
            y * 8 + lax.rem(z + 1, 8), y * 8 + lax.rem(z + 7, 8)]
    root = col == 0
    partner = x * 2 + 1 - core

    barrier = pltpu.get_barrier_semaphore()
    for n in near:
        pl.semaphore_signal(barrier, inc=1, device_id={"pcol": n}, device_id_type=MESH)
    for i in range(1, 8):
        pl.semaphore_signal(barrier, inc=1, device_id={"prow": lax.rem(row + i, 8)}, device_id_type=MESH)

    def load(b):
        rows = pl.ds(pl.multiple_of(b * 128, 128), 128)
        return pltpu.make_async_copy(m_hbm.at[rows], m_ref.at[rows], load_sem.at[b])

    load(0).start()
    get_ui = pltpu.make_async_copy(ui_hbm, ui_ref, in_sem.at[0])
    get_li = pltpu.make_async_copy(li_hbm, li_ref, in_sem.at[1])
    get_piv = pltpu.make_async_copy(piv_hbm, piv_row, in_sem.at[2])
    get_ui.start()
    for b in range(1, 16):
        load(b).start()
    get_piv.start()
    get_li.start()

    trees = pick(OUT_TREE, col)
    depths = pick(DEPTH, col)
    tree = [lax.rem(lax.div(trees, 8**i), 8) for i in range(4)]
    lag = [lax.div(lax.rem(lax.div(depths, 32**i), 32) * HOP, 4) for i in range(4)]
    last_lag = jnp.maximum(jnp.maximum(lag[0], lag[1]), jnp.maximum(lag[2], lag[3]))
    out_lag = [jnp.where(t == 0, lag[0], jnp.where(t == 1, lag[1], jnp.where(t == 2, lag[2], lag[3]))) for t in tree]

    def chunk(t, k):
        return pl.ds(pl.multiple_of(k * (4 * CHUNK) + t * CHUNK, CHUNK), CHUNK)

    def to_row(src, dst, sems, j, target):
        return pltpu.make_async_remote_copy(
            src_ref=src, dst_ref=dst, send_sem=sems[0].at[j], recv_sem=sems[1].at[j],
            device_id={"prow": target}, device_id_type=MESH)

    get_ui.wait()

    @pl.when(root)
    def _():
        tall(ui_tall, ui_ref[...])

    pl.semaphore_wait(barrier, 11)

    mine = pl.ds(pl.multiple_of(core * HALF, HALF), HALF)
    other = pl.ds(pl.multiple_of((1 - core) * HALF, HALF), HALF)
    my_piece = pl.ds(pl.multiple_of(core * HALF + x * PIECE, PIECE), PIECE)
    a_sems = (a_send, a_recv)
    b_sems = (b_send, b_recv)
    a0 = to_row(g_ref.at[other], a0_ref, a_sems, 0, partner)
    a1, a2 = [], []
    for i in range(3):
        peer = lax.rem(x + 3 - i, 4)
        rows = pl.ds(pl.multiple_of(peer * PIECE, PIECE), PIECE)
        a1.append(to_row(h_ref.at[rows], a1_ref.at[i], a_sems, 1 + i, peer * 2 + core))
        a2.append(to_row(nt_ref.at[my_piece], nt_ref.at[my_piece], a_sems, 4 + i, peer * 2 + core))
    a3 = to_row(nt_ref.at[mine], nt_ref.at[mine], a_sems, 7, partner)
    first, second = pl.ds(0, HALF), pl.ds(HALF, HALF)
    quarter = [pl.ds(i * 128, 128) for i in range(4)]

    class Stream:
        def __init__(self, src, dst, sems):
            def part(ref, rows, j, target):
                return to_row(ref.at[rows], dst.at[rows], sems, j, target)

            self.first = [part(src, quarter[i], 1 + i, 2 if i < 2 else 7) for i in range(4)]
            self.rest = [part(src, second, 5, 3), part(src, first, 6, 6), part(src, pl.ds(0, NB), 0, 1)]
            self.relay = [part(dst, quarter[i], 1 + i, 4 if i < 2 else 5) for i in range(4)]
            self.have = {2: ([], first), 7: ([], second), 4: (self.relay[:2], first), 5: (self.relay[2:], second),
                         6: (self.rest[1:2], first), 3: (self.rest[:1], second)}
            self.swap = {d: part(dst, h, 7, d ^ 1) for d, (_, h) in self.have.items()}
            self.back = {d: part(dst, second if h is first else first, 7, d ^ 1) for d, (_, h) in self.have.items()}

        def start(self):
            for c in self.first + self.rest:
                c.start()

        def pass_on(self, i):
            for j, device in ((i, 2), (2 + i, 7)):
                @pl.when(row == device)
                def _(j=j):
                    self.first[j].wait_recv()
                    self.relay[j].start()

        def start_swap(self):
            for d, (waits, _) in self.have.items():
                @pl.when(row == d)
                def _(d=d, waits=waits):
                    for c in waits:
                        c.wait_recv()
                    self.swap[d].start()

        def finish(self):
            for d in self.have:
                @pl.when(row == d)
                def _(d=d):
                    self.swap[d].wait_send()
                    self.back[d].wait_recv()

            @pl.when(row == 1)
            def _():
                self.rest[2].wait_recv()

            @pl.when(row == 0)
            def _():
                for c in self.first + self.rest:
                    c.wait_send()

            for i in range(4):
                @pl.when(row == (2, 7)[i // 2])
                def _(i=i):
                    self.relay[i].wait_send()

    old_top = Stream(m_ref, ot_ref, b_sems)
    old_factor = Stream(l_ref, lo_ref, (c_send, c_recv))
    own_top = pltpu.make_async_copy(m_ref.at[pl.ds(0, NB)], ot_ref, in_sem.at[3])
    own_factor = pltpu.make_async_copy(l_ref.at[pl.ds(0, NB)], lo_ref, in_sem.at[4])
    put_top = pltpu.make_async_copy(top_ref, top_out, u_sem.at[0])
    put_uu = pltpu.make_async_copy(uu_ref, uu_out, u_sem.at[1])
    factor_step = jnp.where(root, 12, last_lag + NB // (4 * CHUNK))

    @pl.when(row == 0)
    def _():
        for b in range(4):
            load(b).wait()
        old_top.start()
        own_top.start()

    for b in range(16):
        @pl.when(jnp.logical_not(root) & ((row > 0) | (b >= 4)))
        def _(b=b):
            load(b).wait()

        if b < 4:
            @pl.when(root & (row > 0))
            def _(b=b):
                load(b).wait()

    get_piv.wait()
    pr = piv_row[...].astype(F32)
    lane = lax.broadcasted_iota(jnp.int32, (1, NB), 1)
    here_at = pr - (row * ROWS).astype(F32)
    here = (pr >= NB) & (here_at >= 0) & (here_at < ROWS)
    here_at = jnp.where(here, here_at, float(2 * ROWS))

    def rank_vacancies():
        vacancy = jnp.where(pr >= NB, 1.0, 0.0)
        for i in range(9):
            vacancy = vacancy + jnp.where(lane >= 2**i, pltpu.roll(vacancy, 2**i, 1), 0.0)
        src_ref[3:4, :] = vacancy

    def column(v):
        return jnp.transpose(jnp.broadcast_to(v, (128, 128)), (1, 0))[:, :1]

    pl.when(jnp.logical_not(root))(rank_vacancies)

    def body(s, carry):
        pl.when(root & (s == 17))(rank_vacancies)

        @pl.when(root & (s < 16))
        def _():
            @pl.when(s == 3)
            def _():
                for b in range(4, 16):
                    load(b).wait()

            rows = pl.ds(pl.multiple_of(s * 128, 128), 128)
            l_ref[rows, :] = product(m_ref[rows, :NB], ui_tall)

        @pl.when(root & (s >= 1) & (s <= 16))
        def _():
            for u in range(2):
                k = 2 * (s - 1) + u
                for d in range(4):
                    @pl.when(tree[d] < 4)
                    def _(d=d, k=k):
                        part = l_ref.at[chunk(tree[d], k)]
                        pltpu.make_async_remote_copy(
                            src_ref=part, dst_ref=part, send_sem=send_sem.at[d, k], recv_sem=recv_sem.at[tree[d], k],
                            device_id={"pcol": near[d]}, device_id_type=MESH).start()

        @pl.when(jnp.logical_not(root))
        def _():
            for t in range(4):
                k = s - lag[t]

                @pl.when((k >= 0) & (k < CHUNKS))
                def _(t=t, k=k):
                    part = l_ref.at[chunk(t, k)]
                    pltpu.make_async_copy(part, part, recv_sem.at[t, k]).wait()

            for d in range(4):
                k = s - out_lag[d]

                @pl.when((tree[d] < 4) & (k >= 0) & (k < CHUNKS))
                def _(d=d, k=k):
                    part = l_ref.at[chunk(tree[d], k)]
                    pltpu.make_async_remote_copy(
                        src_ref=part, dst_ref=part, send_sem=send_sem.at[d, k], recv_sem=recv_sem.at[tree[d], k],
                        device_id={"pcol": near[d]}, device_id_type=MESH).start()

            for t in range(4):
                k = s - lag[t]

                @pl.when((k >= 0) & (k < CHUNKS))
                def _(t=t, k=k):
                    pltpu.make_async_copy(l_ref.at[chunk(t, k)], l_out.at[chunk(t, k)], out_sem).start()

        @pl.when((s == factor_step) & (row == 0))
        def _():
            old_factor.start()
            own_factor.start()

        for i in range(2):
            @pl.when(s == factor_step + 11 + 4 * i)
            def _(i=i):
                old_factor.pass_on(i)

            @pl.when(s == 14 + 4 * i)
            def _(i=i):
                old_top.pass_on(i)

        @pl.when(s == 36)
        def _():
            old_top.start_swap()

        at_step = s - jnp.where(root, ROOT_LATE, 0)

        @pl.when((at_step >= 0) & (at_step < GATHER_STEPS))
        def _():
            for i in range(NB // GATHER_STEPS):
                j = lax.rem(at_step * (NB // GATHER_STEPS) + (1 - core) * HALF, NB) + i
                at = piv[j] - row * ROWS
                inside = (at >= 0) & (at < ROWS)
                picked = m_ref[pl.ds(jnp.clip(at, 0, ROWS - 1), 1), :]
                g_ref[pl.ds(j, 1), :] = jnp.where(inside, picked, 0.0)

        def step(n):
            return pl.when(at_step == n)

        @step(9)
        def _():
            a0.start()

        @step(17)
        def _():
            a0.wait()
            h_ref[...] = g_ref[mine, :] + a0_ref[...]

        @step(18)
        def _():
            for c in a1:
                c.start()

        for q in range(4):
            @step(20 + q)
            def _(q=q):
                vacancy = src_ref[3:4, :]
                slot = (lax.broadcasted_iota(jnp.int32, (128, 1), 0) + 128 * q).astype(F32)
                chosen = jnp.sum(jnp.where(pr == slot, 1.0, 0.0), axis=1, keepdims=True)
                rank = slot - jnp.sum(jnp.where(pr <= slot, 1.0, 0.0), axis=1, keepdims=True)
                key = jnp.where(chosen > 0, -7.0, rank)
                found = jnp.sum(jnp.where(key == vacancy - 1, slot, 0.0), axis=0, keepdims=True)
                src_ref[0:1, :] = found if q == 0 else src_ref[0:1, :] + found

        for q in range(4):
            @step(24 + q)
            def _(q=q):
                cut = slice(128 * q, 128 * q + 128)
                at_col = column(here_at[:, cut])
                src_col = column(src_ref[0:1, cut])
                place = jnp.sum(jnp.where(here_at < at_col, 1.0, 0.0), axis=1, keepdims=True)
                place = jnp.where(at_col < ROWS, place, -7.0)
                code = jnp.sum(jnp.where(place == lane.astype(F32), at_col * NB + src_col, 0.0), axis=0, keepdims=True)
                edge = (lane[:, :128] * TILE).astype(F32)
                count = jnp.sum(jnp.where(at_col < edge, 1.0, 0.0), axis=0, keepdims=True)
                src_ref[1:2, :] = code if q == 0 else src_ref[1:2, :] + code
                src_ref[2:3, :128] = count if q == 0 else src_ref[2:3, :128] + count
                if q == 3:
                    list_ref[...] = src_ref[1:2, :].astype(jnp.int32)
                    bound_ref[...] = src_ref[2:3, :128].astype(jnp.int32)

        @step(38)
        def _():
            for c in a1:
                c.wait()
            nt_ref[my_piece, :] = h_ref[pl.ds(pl.multiple_of(x * PIECE, PIECE), PIECE), :] + a1_ref[0] + a1_ref[1] + a1_ref[2]

        @step(39)
        def _():
            for c in a2:
                c.start()

        @step(52)
        def _():
            for c in a2:
                c.wait()
            a3.start()

        @step(56)
        def _():
            a3.wait()
            get_li.wait()
            tall(nt_tall, nt_ref[...])

        for q in range(4):
            @step(57 + q)
            def _(q=q):
                cut = slice(128 * q, 128 * q + 128)
                u = product(li_ref[cut, :], nt_tall)
                top_ref[cut, :] = u
                tall(uu_ref, u, 128 * q)

                @pl.when(root)
                def _():
                    top_ref[cut, :NB] = nt_ref[cut, :NB]

        @step(61)
        def _():
            put_top.start()
            put_uu.start()

        return carry

    lax.fori_loop(0, STEPS + 1 + jnp.where(root, ROOT_LATE, 0), body, 0)

    @pl.when(root)
    def _():
        pltpu.make_async_copy(l_ref, l_out, out_sem).start()

    old_factor.start_swap()
    old_top.finish()
    old_factor.finish()

    @pl.when(row == 0)
    def _():
        own_top.wait()
        own_factor.wait()

    put_top.wait()
    put_uu.wait()

    def drain(k, carry):
        for d in range(4):
            @pl.when(tree[d] < 4)
            def _(d=d):
                part = l_ref.at[chunk(tree[d], k)]
                pltpu.make_async_copy(part, part, send_sem.at[d, k]).wait()
        return carry

    lax.fori_loop(0, CHUNKS, drain, 0)
    pltpu.make_async_copy(l_ref, l_out, out_sem).wait()


def update(code, bounds, m_ref, l_ref, uu_ref, top_ref, ot_ref, lo_ref, o_ref, lt_ref):
    b = pl.program_id(0)
    row = lax.axis_index("prow")
    col = lax.axis_index("pcol")
    top = (row == 0) & (b < NB // TILE)

    @pl.when(top)
    def _():
        o_ref[...] = top_ref[...]

    @pl.when(jnp.logical_not(top))
    def _():
        o_ref[...] = m_ref[...]
        lt_ref[...] = l_ref[...]

        def place(p, carry):
            at, source = lax.div(code[0, p], NB), lax.rem(code[0, p], NB)
            here, there = pl.ds(at - b * TILE, 1), pl.ds(source, 1)
            o_ref[here, :] = ot_ref[there, :]
            lt_ref[here, :] = lo_ref[there, :]
            return carry

        lax.fori_loop(bounds[0, b], bounds[0, b + 1], place, 0)
        o_ref[...] = o_ref[...] - product(lt_ref[...], uu_ref)

        @pl.when(col == 0)
        def _():
            o_ref[:, :NB] = lt_ref[...]


def local(matrix, pivots, lower_inverse, upper_inverse):
    vmem = pl.BlockSpec(memory_space=pltpu.VMEM)
    hbm = pl.BlockSpec(memory_space=pl.ANY)
    stay = pl.BlockSpec(memory_space=pltpu.MemorySpace.HBM)
    strip = jax.ShapeDtypeStruct((NB, COLS), F32)
    u_tall = jax.ShapeDtypeStruct((3 * NB, COLS), BF16)
    spread, top, u_tall, old, old_factor, code, bounds = pl.pallas_call(
        exchange,
        out_shape=(jax.ShapeDtypeStruct((ROWS, NB), F32), strip, u_tall, strip, jax.ShapeDtypeStruct((NB, NB), F32),
                   jax.ShapeDtypeStruct((1, NB), jnp.int32), jax.ShapeDtypeStruct((1, 128), jnp.int32)),
        in_specs=[pl.BlockSpec(memory_space=pltpu.SMEM), stay, stay, stay, stay],
        out_specs=(hbm, hbm, hbm, hbm, hbm, vmem, vmem),
        scratch_shapes=[
            pltpu.VMEM((ROWS, COLS), F32),
            pltpu.VMEM((ROWS, NB), F32),
            pltpu.VMEM((NB, COLS), F32),
            pltpu.VMEM((HALF, COLS), F32),
            pltpu.VMEM((HALF, COLS), F32),
            pltpu.VMEM((3, PIECE, COLS), F32),
            pltpu.VMEM((NB, COLS), F32),
            pltpu.VMEM((3 * NB, NB), BF16),
            pltpu.VMEM((3 * NB, COLS), BF16),
            pltpu.VMEM((8, NB), F32),
            pltpu.VMEM((1, NB), jnp.int32),
            pltpu.VMEM((NB, NB), F32),
            pltpu.VMEM((NB, NB), F32),
            pltpu.VMEM((NB, COLS), F32),
            pltpu.VMEM((3 * NB, COLS), BF16),
            pltpu.SemaphoreType.DMA((16,)),
            pltpu.SemaphoreType.DMA((5,)),
            pltpu.SemaphoreType.DMA((4, CHUNKS)),
            pltpu.SemaphoreType.DMA((4, CHUNKS)),
            pltpu.SemaphoreType.DMA,
            pltpu.SemaphoreType.DMA((2,)),
            *[pltpu.SemaphoreType.DMA((8,))] * 6,
        ],
        compiler_params=pltpu.CompilerParams(collective_id=0, has_side_effects=True, vmem_limit_bytes=EXCHANGE_VMEM),
        name="exchange",
    )(pivots, pivots.reshape(1, NB), *(pltpu.with_memory_space_constraint(v, pltpu.MemorySpace.HBM) for v in (matrix, lower_inverse, upper_inverse)))
    tile = lambda width: pl.BlockSpec((TILE, width), lambda b, *_: (b, 0))
    whole = lambda rows: pl.BlockSpec((rows, COLS), lambda b, *_: (0, 0))
    return pl.pallas_call(
        update,
        out_shape=jax.ShapeDtypeStruct((ROWS, COLS), F32),
        grid_spec=pltpu.PrefetchScalarGridSpec(
            num_scalar_prefetch=2,
            grid=(ROWS // TILE,),
            in_specs=[tile(COLS), tile(NB), whole(3 * NB), whole(NB), whole(NB), pl.BlockSpec((NB, NB), lambda b, *_: (0, 0))],
            out_specs=tile(COLS),
            scratch_shapes=[pltpu.VMEM((TILE, NB), F32)],
        ),
        compiler_params=pltpu.CompilerParams(vmem_limit_bytes=UPDATE_VMEM),
        name="update",
    )(code, bounds, matrix, spread, u_tall, top, old, old_factor)


def solution(mesh):
    return jax.shard_map(
        local,
        mesh=mesh,
        in_specs=(P("prow", "pcol"), P(), P(), P()),
        out_specs=P("prow", "pcol"),
        check_vma=False,
    )
```
